32 devices in a mesh: groups: 2 (over y), tile: 8 (over z, x), col: 2 (over core).
Axes of the slice: x: 2, y: 2, z: 4, core: 2. Of those that a mesh axis runs over, the one named last changes fastest.
Arguments:
- jacobian: bfloat16 [512, 3, 128, 512], P(('groups', 'tile'), None, None, 'col'), parts along dimension 0, may hold values from -0.15625 to 0.15625
- footprint: int32 [512, 3], P(('groups', 'tile')), parts along dimension 0, may hold values from 0 to 4, all different within a row
- live: int32 [16], P(('groups', 'tile')), parts along dimension 0, may hold values from 1 to 32, as said below
- noise_weight: float32 [512, 128], P(('groups', 'tile')), parts along dimension 0, may hold values from 0.25 to 4
- probes: bfloat16 [16, 512, 256], P(('groups', 'tile'), 'col'), parts along dimension 0, may hold values from -6 to 6
Outputs:
- basis: float32 [16, 512, 256], P(('groups', 'tile'), 'col'), parts along dimension 0
- factor: float32 [512, 256], P('groups'), parts along dimension 0
The draws below stay inside these ranges and needn't reach their ends.
There are 2 independent parts, one for each index of `groups`. The reference program is written for one: setup_inputs(seed, part) draws one part's arguments, and reference() takes and returns one part's arrays. A program takes and returns all parts, laid end to end along the dimension named above; each array names one. Nothing has to cross between parts.
Inputs may be any that keep to these rules, and one draw needn't show every extreme that they name: `footprint`: each row lists 3 different offsets. Some band has all 32 slots live.
All inputs are finite; a program needn't handle non-finite values.
Results may differ from the reference program's by a relative error of at most 0.0014.
Values may be sent and summed in bfloat16 or wider, within the bound.
A program may use at most 64 MiB of HBM per device.

```python
import math
import jax
import jax.numpy as jnp
from jax import lax

PROBES = 256
TOUCHED = 3
BLOCK_ROWS = 128
SLOTS = 32
BANDS = 8
TILE_CELLS = 512
BLOCKS = 256


def draw_live(key, part):
    counts = jax.random.randint(key, (BANDS,), 1, SLOTS + 1)
    where = jax.random.randint(jax.random.fold_in(key, 7), (), 0, BANDS)
    return counts.at[where].set(SLOTS).astype(jnp.int32)


def block_levels(own_key, extent, split, low, high):
    def one(dim, parts):
        steps = jax.random.uniform(jax.random.fold_in(jax.random.fold_in(own_key, 6), dim), (parts,), jnp.float32, low / len(split), high / len(split))
        return jnp.repeat(jnp.exp(steps), extent[dim] // parts).reshape((-1,) + (1,) * (len(extent) - dim - 1))

    factor_of = one(*split[0])
    for cut in split[1:]:
        factor_of = factor_of * one(*cut)
    return factor_of


def different_ones(own_key, rows, number_of, top, lift):
    ranking = jax.random.permutation(jax.random.fold_in(own_key, 1), number_of)
    boost = ranking
    for power in range(3):
        boost = boost * boost // number_of
    boost = boost * lift // number_of
    lots = jax.random.randint(jax.random.fold_in(own_key, 2), (rows, number_of), 0, 4096) + boost
    sure = jax.random.permutation(jax.random.fold_in(own_key, 3), rows)[jnp.arange(number_of) % rows]
    lots = jnp.where(jnp.arange(rows)[:, None] == sure[None, :], 1 << 14, lots)
    merit = lots * number_of + jnp.arange(number_of)
    return lax.top_k(merit.astype(jnp.int32), top)[1].astype(jnp.int32)


def centred(own_key, dims, scale, reach, shards=(), kind=jnp.bfloat16):
    loudness = block_levels(own_key, dims, shards, -0.22, 0.18) if shards else 1.0
    array = jax.random.normal(own_key, dims, jnp.float32) * scale * loudness
    return jnp.minimum(jnp.maximum(array, -reach), reach).astype(kind)


def setup_inputs(seed: int = 0, part: int = 0) -> dict:
    streams_of = jax.random.split(jax.random.key(seed), 6)
    part_keys = jax.random.split(jax.random.fold_in(streams_of[5], part), 6)
    return {
        "jacobian": centred(part_keys[0], (BLOCKS, TOUCHED, BLOCK_ROWS, TILE_CELLS), (TOUCHED * TILE_CELLS) ** -0.5, 0.15625, ((0, 8), (3, 2))),
        "footprint": different_ones(part_keys[1], BLOCKS, 5, TOUCHED, 0),
        "live": draw_live(jax.random.fold_in(jax.random.fold_in(streams_of[5], part), 71), part),
        "noise_weight": jnp.clip(jnp.exp(math.log(4.0) - 2.7725887 * jax.random.uniform(part_keys[3], (BLOCKS, BLOCK_ROWS), jnp.float32) ** block_levels(part_keys[3], (BLOCKS, BLOCK_ROWS), ((0, 8),), -0.2, 0.2)), 0.25, 4.0),
        "probes": centred(part_keys[4], (BANDS, TILE_CELLS, PROBES), 1.0, 6.0, ((0, 8), (1, 2))),
    }


def reference(jacobian, footprint, live, noise_weight, probes):
    bands, tile_cells, width = probes.shape
    blocks_all = jacobian.reshape(bands, SLOTS, TOUCHED, BLOCK_ROWS, tile_cells)
    foot_all = footprint.reshape(bands, SLOTS, TOUCHED)
    weight_all = noise_weight.reshape(bands, SLOTS, BLOCK_ROWS)
    probe_full = probes.astype(jnp.float32)
    offsets = jnp.arange(5, dtype=jnp.int32) - 2

    def band_step(total, band):
        foot_here = foot_all[band]
        tiles = (band + foot_here - 2) % bands
        picked = probe_full[tiles]
        block = blocks_all[band].astype(jnp.float32)
        images = jnp.einsum('sfrc,sfck->srk', block, picked)
        active = (jnp.arange(SLOTS, dtype=jnp.int32) < live[band]).astype(jnp.float32)
        scaling = weight_all[band] * active[:, None]
        weighted = (images * scaling[:, :, None]).astype(jnp.bfloat16)
        weighted = lax.optimization_barrier(weighted).astype(jnp.float32)
        contrib = jnp.einsum('sfrc,srk->sfck', block, weighted)
        onehot = (foot_here[:, :, None] == jnp.arange(5, dtype=jnp.int32)[None, None, :]).astype(jnp.float32)
        bucket = jnp.einsum('sfo,sfck->ock', onehot, contrib, precision=lax.Precision.HIGHEST)
        return (total.at[(band + offsets) % bands].add(bucket), None)
    total, _ = lax.scan(band_step, jnp.zeros_like(probe_full), jnp.arange(bands, dtype=jnp.int32))
    sketch = (probe_full + total).reshape(bands * tile_cells, width)
    gram = jnp.dot(sketch.T, sketch, precision=lax.Precision.HIGHEST)
    lower = jnp.linalg.cholesky(gram)
    scale = jnp.sqrt(jnp.float32(bands * tile_cells))
    solved = jax.scipy.linalg.solve_triangular(lower, sketch.T, lower=True)
    basis = (solved.T * scale).reshape(bands, tile_cells, width)
    factor = lower.T / scale
    return (basis, factor)
```

```python
import functools
import math

import jax
import jax.numpy as jnp
from jax import lax
from jax.experimental import pallas as pl
from jax.experimental.pallas import tpu as pltpu
from jax.sharding import PartitionSpec as P

MESH = pl.DeviceIdType.MESH
REACH = 5
VMEM = pl.BlockSpec(memory_space=pltpu.VMEM)
ANY = pl.BlockSpec(memory_space=pl.ANY)
HIGHEST = lax.Precision.HIGHEST


def remote(src, dst, send, recv, where):
    return pltpu.make_async_remote_copy(
        src_ref=src, dst_ref=dst, send_sem=send, recv_sem=recv,
        device_id=where, device_id_type=MESH,
    )


def greet(devices):
    barrier = pltpu.get_barrier_semaphore()
    for where in devices:
        pl.semaphore_signal(barrier, inc=1, device_id=where, device_id_type=MESH)
    pl.semaphore_wait(barrier, len(devices))


def ring(bands):
    me = lax.axis_index("tile")
    odd = lax.rem(me, 2)
    mate = me + 1 - 2 * odd
    up = lax.rem(me + 2, bands)
    down = lax.rem(me + bands - 2, bands)
    return me, odd, mate, up, down


def window_kernel(bands, probes, window, send, recv):
    me, odd, mate, up, down = ring(bands)
    greet([{"tile": mate}, {"tile": up}, {"tile": down}])
    own = probes.at[0]
    hops = [
        remote(own, window.at[0], send.at[0], recv.at[0], {"tile": up}),
        remote(own, window.at[4], send.at[1], recv.at[1], {"tile": down}),
        remote(own, window.at[1 + 2 * odd], send.at[2], recv.at[2], {"tile": mate}),
        remote(window.at[4 - 4 * odd], window.at[3 - 2 * odd], send.at[3], recv.at[3], {"tile": mate}),
    ]
    for hop in hops[:3]:
        hop.start()
    window[2] = probes[0]
    hops[0].wait_recv()
    hops[1].wait_recv()
    hops[3].start()
    hops[2].wait_recv()
    hops[3].wait_recv()
    for hop in hops:
        hop.wait_send()


def fetch_window(probes, bands):
    _, cells, width = probes.shape
    return pl.pallas_call(
        functools.partial(window_kernel, bands),
        out_shape=jax.ShapeDtypeStruct((REACH, cells, width), probes.dtype),
        in_specs=[VMEM],
        out_specs=VMEM,
        scratch_shapes=[pltpu.SemaphoreType.DMA((4,)), pltpu.SemaphoreType.DMA((4,))],
        compiler_params=pltpu.CompilerParams(collective_id=0, has_side_effects=True),
        name="fetch_window",
    )(probes)


def forward_kernel(group, reach, foot, jac, window, out, turned):
    step = pl.program_id(0)

    @pl.when(step == 0)
    def _():
        for o in range(REACH):
            turned[o] = window[o].astype(jnp.float32).T.astype(turned.dtype)

    for g in range(group):
        total = None
        for f in range(reach):
            o = foot[(step * group + g) * reach + f]
            part = lax.dot_general(
                turned[o], jac[g, f], (((1,), (1,)), ((), ())), preferred_element_type=jnp.float32
            )
            total = part if total is None else total + part
        out[g] = total


def forward(foot, jacobian, window, group):
    slots, reach, rows, cells = jacobian.shape
    width = window.shape[2]
    return pl.pallas_call(
        functools.partial(forward_kernel, group, reach),
        out_shape=jax.ShapeDtypeStruct((slots, width, rows), jnp.float32),
        grid_spec=pltpu.PrefetchScalarGridSpec(
            num_scalar_prefetch=1,
            grid=(slots // group,),
            in_specs=[
                pl.BlockSpec((group, reach, rows, cells), lambda i, foot: (i, 0, 0, 0)),
                pl.BlockSpec((REACH, cells, width), lambda i, foot: (0, 0, 0)),
            ],
            out_specs=pl.BlockSpec((group, width, rows), lambda i, foot: (i, 0, 0)),
            scratch_shapes=[pltpu.VMEM((REACH, width, cells), window.dtype)],
        ),
        name="forward_images",
    )(foot, jacobian, window)


def swap_kernel(value, other, send, recv):
    partner = {"col": 1 - lax.axis_index("col")}
    greet([partner])
    hop = remote(value, other, send, recv, partner)
    hop.start()
    hop.wait()


def swap_cores(value):
    return pl.pallas_call(
        swap_kernel,
        out_shape=jax.ShapeDtypeStruct(value.shape, value.dtype),
        in_specs=[ANY],
        out_specs=ANY,
        scratch_shapes=[pltpu.SemaphoreType.DMA, pltpu.SemaphoreType.DMA],
        compiler_params=pltpu.CompilerParams(collective_id=1, has_side_effects=True),
        name="swap_images",
    )(value)


def backward_kernel(group, reach, foot, live, jac, noise, mine, other, bucket):
    step = pl.program_id(0)

    @pl.when(step == 0)
    def _():
        bucket[...] = jnp.zeros_like(bucket)

    for g in range(group):
        slot = step * group + g
        active = jnp.where(slot < live[0], 1.0, 0.0).astype(jnp.float32)
        scale = noise[pl.ds(slot, 1), :] * active
        weighted = ((mine[g] + other[g]) * scale).astype(jnp.bfloat16)
        for f in range(reach):
            o = foot[slot * reach + f]
            bucket[o] += jnp.dot(weighted, jac[g, f], preferred_element_type=jnp.float32)


def backward(foot, live, jacobian, noise, mine, other, group):
    slots, reach, rows, cells = jacobian.shape
    width = mine.shape[1]
    return pl.pallas_call(
        functools.partial(backward_kernel, group, reach),
        out_shape=jax.ShapeDtypeStruct((REACH, width, cells), jnp.float32),
        grid_spec=pltpu.PrefetchScalarGridSpec(
            num_scalar_prefetch=2,
            grid=(slots // group,),
            in_specs=[
                pl.BlockSpec((group, reach, rows, cells), lambda i, foot, live: (i, 0, 0, 0)),
                pl.BlockSpec((slots, rows), lambda i, foot, live: (0, 0)),
                pl.BlockSpec((group, width, rows), lambda i, foot, live: (i, 0, 0)),
                pl.BlockSpec((group, width, rows), lambda i, foot, live: (i, 0, 0)),
            ],
            out_specs=pl.BlockSpec((REACH, width, cells), lambda i, foot, live: (0, 0, 0)),
        ),
        name="back_project",
    )(foot, live, jacobian, noise, mine, other)


def collect_kernel(bands, split, bucket, probes, field, gram, got, relay, half, mine, parts, full, whole,
                   send, recv, gsend, grecv, asend, arecv):
    me, odd, mate, up, down = ring(bands)
    core = lax.axis_index("col")
    partner = {"col": 1 - core}
    peers = [{"tile": lax.rem(me + d, bands)} for d in range(1, bands)]
    greet(peers + [partner])
    straight = {"tile": lax.rem(me + bands - 2 + 4 * odd, bands)}
    turned = {"tile": lax.rem(me + 2 + (bands - 4) * odd, bands)}
    hops = [
        remote(bucket.at[1 + 2 * odd], got.at[0], send.at[0], recv.at[0], {"tile": mate}),
        remote(bucket.at[4 * odd], got.at[2], send.at[1], recv.at[1], straight),
        remote(bucket.at[3 - 2 * odd], got.at[1], send.at[2], recv.at[2], {"tile": mate}),
        remote(relay, got.at[3], send.at[3], recv.at[3], turned),
    ]
    for hop in hops[:3]:
        hop.start()
    base = probes[0].astype(jnp.float32).T + bucket[2]
    hops[0].wait_recv()
    relay[...] = bucket[4 - 4 * odd] + got[0]
    hops[3].start()
    hops[2].wait_recv()
    base = base + got[1]
    hops[1].wait_recv()
    base = base + got[2]
    hops[3].wait_recv()
    field[...] = base + got[3]
    for hop in hops:
        hop.wait_send()
    value = field[...]
    local = lax.dot_general(
        value, value, (((1,), (1,)), ((), ())), precision=HIGHEST, preferred_element_type=jnp.float32
    )
    if not split:
        gram[...] = local
        return
    rows = half.shape[1]
    piece = rows // bands
    whole[0] = local[:rows]
    whole[1] = local[rows:]
    hop = remote(whole.at[1 - core], half.at[0], gsend.at[0], grecv.at[0], partner)
    hop.start()
    hop.wait()
    mine[...] = (whole[core] + half[0]).reshape(bands, piece, mine.shape[2])
    hops = []
    for d in range(1, bands):
        target = lax.rem(me + d, bands)
        hops.append(remote(mine.at[target], parts.at[d - 1], gsend.at[d], grecv.at[d], {"tile": target}))
    for hop in hops:
        hop.start()
    total = mine[me]
    for d in range(1, bands):
        hops[d - 1].wait_recv()
        total = total + parts[d - 1]
    for hop in hops:
        hop.wait_send()
    full[me] = total
    hops = []
    for d in range(1, bands):
        target = lax.rem(me + d, bands)
        hops.append(remote(full.at[me], full.at[me], asend.at[d], arecv.at[d], {"tile": target}))
    for hop in hops:
        hop.start()
    for hop in hops:
        hop.wait_recv()
    for hop in hops:
        hop.wait_send()
    hop = remote(full, gram.at[core], asend.at[0], arecv.at[0], partner)
    hop.start()
    gram[core] = full[...]
    hop.wait()


def collect(bucket, probes, bands, split):
    _, width, cells = bucket.shape
    rows = width // 2
    piece = rows // bands if split else 8
    gram_shape = (2, bands, piece, width) if split else (width, width)
    field, gram = pl.pallas_call(
        functools.partial(collect_kernel, bands, split),
        out_shape=(
            jax.ShapeDtypeStruct((width, cells), jnp.float32),
            jax.ShapeDtypeStruct(gram_shape, jnp.float32),
        ),
        in_specs=[VMEM, VMEM],
        out_specs=(VMEM, VMEM),
        scratch_shapes=[
            pltpu.VMEM((4, width, cells), jnp.float32),
            pltpu.VMEM((width, cells), jnp.float32),
            pltpu.VMEM((1, rows, width), jnp.float32),
            pltpu.VMEM((bands, piece, width), jnp.float32),
            pltpu.VMEM((bands - 1, piece, width), jnp.float32),
            pltpu.VMEM((bands, piece, width), jnp.float32),
            pltpu.VMEM((2, rows, width), jnp.float32),
            pltpu.SemaphoreType.DMA((4,)),
            pltpu.SemaphoreType.DMA((4,)),
            pltpu.SemaphoreType.DMA((bands,)),
            pltpu.SemaphoreType.DMA((bands,)),
            pltpu.SemaphoreType.DMA((bands,)),
            pltpu.SemaphoreType.DMA((bands,)),
        ],
        compiler_params=pltpu.CompilerParams(collective_id=2, has_side_effects=True),
        name="collect_gram",
    )(bucket, probes)
    return field, gram.reshape(width, width)


def eliminate(block):
    size = block.shape[0]
    groups = [block[8 * g : 8 * g + 8] for g in range(size // 8)]
    sub = lax.broadcasted_iota(jnp.int32, (8, 1), 0)
    for g in range(len(groups)):
        panel = groups[g]
        scaled = []
        for i in range(8):
            j = 8 * g + i
            r = lax.rsqrt(panel[i : i + 1, j : j + 1])
            upper = panel[i : i + 1, :] * r
            factor = jnp.where(sub > i, panel[:, j : j + 1] * r, 0.0)
            panel = jnp.where(sub == i, upper, panel - factor * upper)
            scaled.append((j, r, upper))
        groups[g] = panel
        for h in range(g + 1, len(groups)):
            rest = groups[h]
            for j, r, upper in scaled:
                rest = rest - (rest[:, j : j + 1] * r) * upper
            groups[h] = rest
    return jnp.concatenate(groups, axis=0)


def finish_kernel(scale, gram, field, basis, factor, inverse):
    width = gram.shape[0]
    half = width // 2
    row = lax.broadcasted_iota(jnp.int32, (half, half), 0)
    lane = lax.broadcasted_iota(jnp.int32, (half, half), 1)
    unit = jnp.where(row == lane, 1.0, 0.0).astype(jnp.float32)
    keep = lane >= row
    zeros = jnp.zeros((half, half), jnp.float32)
    top = eliminate(jnp.concatenate([gram[:half, :], unit], axis=1))
    side = top[:, half:width]
    inverse[:half, :half] = top[:, width:]
    inverse[:half, half:] = zeros
    factor[:half, :half] = jnp.where(keep, top[:, :half], 0.0) * (1.0 / scale)
    factor[:half, half:] = side * (1.0 / scale)
    change = jnp.dot(side.T, top[:, half:], precision=HIGHEST, preferred_element_type=jnp.float32)
    low = eliminate(
        jnp.concatenate([gram[half:, half:] - change[:, :half], -change[:, half:], unit], axis=1)
    )
    inverse[half:, :] = low[:, half:]
    factor[half:, half:] = jnp.where(keep, low[:, :half], 0.0) * (1.0 / scale)
    factor[half:, :half] = zeros
    solved = jnp.dot(inverse[...], field[...], precision=HIGHEST, preferred_element_type=jnp.float32)
    basis[0] = (solved * scale).T


def finish(gram, field, scale):
    width, cells = field.shape
    return pl.pallas_call(
        functools.partial(finish_kernel, scale),
        out_shape=(
            jax.ShapeDtypeStruct((1, cells, width), jnp.float32),
            jax.ShapeDtypeStruct((width, width), jnp.float32),
        ),
        in_specs=[VMEM, VMEM],
        out_specs=(VMEM, VMEM),
        scratch_shapes=[pltpu.VMEM((width, width), jnp.float32)],
        name="factor_solve",
    )(gram, field)


def on_device(jacobian, footprint, live, noise_weight, probes):
    slots = jacobian.shape[0]
    cells, width = probes.shape[1:]
    bands = lax.axis_size("tile")
    group = math.gcd(slots, 4)
    foot = footprint.reshape(-1)
    split = (width // 2) % (8 * bands) == 0
    window = fetch_window(probes, bands)
    mine = forward(foot, jacobian, window, group)
    other = swap_cores(mine)
    bucket = backward(foot, live, jacobian, noise_weight, mine, other, group)
    field, gram = collect(bucket, probes, bands, split)
    if not split:
        gram = lax.psum(gram, ("tile", "col"))
    scale = math.sqrt(cells * lax.axis_size("col") * bands)
    return finish(gram, field, scale)


def solution(mesh):
    placed = (
        P(("groups", "tile"), None, None, "col"),
        P(("groups", "tile"), None),
        P(("groups", "tile")),
        P(("groups", "tile"), None),
        P(("groups", "tile"), "col", None),
    )
    return jax.shard_map(
        on_device,
        mesh=mesh,
        in_specs=placed,
        out_specs=(P(("groups", "tile"), "col", None), P("groups", None)),
        check_vma=False,
    )
```

```python
import functools
import math

import jax
import jax.numpy as jnp
from jax import lax
from jax.experimental import pallas as pl
from jax.experimental.pallas import tpu as pltpu
from jax.sharding import PartitionSpec as P

MESH = pl.DeviceIdType.MESH
REACH = 5
LEVELS = 32766.0
VMEM = pl.BlockSpec(memory_space=pltpu.VMEM)
ANY = pl.BlockSpec(memory_space=pl.ANY)
HIGHEST = lax.Precision.HIGHEST


def remote(src, dst, send, recv, where):
    return pltpu.make_async_remote_copy(
        src_ref=src, dst_ref=dst, send_sem=send, recv_sem=recv,
        device_id=where, device_id_type=MESH,
    )


def greet(devices):
    barrier = pltpu.get_barrier_semaphore()
    for where in devices:
        pl.semaphore_signal(barrier, inc=1, device_id=where, device_id_type=MESH)
    pl.semaphore_wait(barrier, len(devices))


def ring(bands):
    me = lax.axis_index("tile")
    odd = lax.rem(me, 2)
    mate = me + 1 - 2 * odd
    up = lax.rem(me + 2, bands)
    down = lax.rem(me + bands - 2, bands)
    return me, odd, mate, up, down


def window_kernel(bands, probes, window, send, recv):
    me, odd, mate, up, down = ring(bands)
    greet([{"tile": mate}, {"tile": up}, {"tile": down}])
    own = probes.at[0]
    hops = [
        remote(own, window.at[0], send.at[0], recv.at[0], {"tile": up}),
        remote(own, window.at[4], send.at[1], recv.at[1], {"tile": down}),
        remote(own, window.at[1 + 2 * odd], send.at[2], recv.at[2], {"tile": mate}),
        remote(window.at[4 - 4 * odd], window.at[3 - 2 * odd], send.at[3], recv.at[3], {"tile": mate}),
    ]
    for hop in hops[:3]:
        hop.start()
    window[2] = probes[0]
    hops[0].wait_recv()
    hops[1].wait_recv()
    hops[3].start()
    hops[2].wait_recv()
    hops[3].wait_recv()
    for hop in hops:
        hop.wait_send()


def fetch_window(probes, bands):
    _, cells, width = probes.shape
    return pl.pallas_call(
        functools.partial(window_kernel, bands),
        out_shape=jax.ShapeDtypeStruct((REACH, cells, width), probes.dtype),
        in_specs=[VMEM],
        out_specs=VMEM,
        scratch_shapes=[pltpu.SemaphoreType.DMA((4,)), pltpu.SemaphoreType.DMA((4,))],
        compiler_params=pltpu.CompilerParams(collective_id=0, has_side_effects=True),
        name="fetch_window",
    )(probes)


def forward_kernel(group, reach, foot, jac, window, out, turned):
    step = pl.program_id(0)

    @pl.when(step == 0)
    def _():
        for o in range(REACH):
            turned[o] = window[o].astype(jnp.float32).T.astype(turned.dtype)

    for g in range(group):
        total = None
        for f in range(reach):
            o = foot[(step * group + g) * reach + f]
            part = lax.dot_general(
                turned[o], jac[g, f], (((1,), (1,)), ((), ())), preferred_element_type=jnp.float32
            )
            total = part if total is None else total + part
        out[g] = total


def forward(foot, jacobian, window, group):
    slots, reach, rows, cells = jacobian.shape
    width = window.shape[2]
    return pl.pallas_call(
        functools.partial(forward_kernel, group, reach),
        out_shape=jax.ShapeDtypeStruct((slots, width, rows), jnp.float32),
        grid_spec=pltpu.PrefetchScalarGridSpec(
            num_scalar_prefetch=1,
            grid=(slots // group,),
            in_specs=[
                pl.BlockSpec((group, reach, rows, cells), lambda i, foot: (i, 0, 0, 0)),
                pl.BlockSpec((REACH, cells, width), lambda i, foot: (0, 0, 0)),
            ],
            out_specs=pl.BlockSpec((group, width, rows), lambda i, foot: (i, 0, 0)),
            scratch_shapes=[pltpu.VMEM((REACH, width, cells), window.dtype)],
        ),
        name="forward_images",
    )(foot, jacobian, window)


def swap_kernel(value, other, send, recv):
    partner = {"col": 1 - lax.axis_index("col")}
    greet([partner])
    hop = remote(value, other, send, recv, partner)
    hop.start()
    hop.wait()


def swap_cores(value):
    return pl.pallas_call(
        swap_kernel,
        out_shape=jax.ShapeDtypeStruct(value.shape, value.dtype),
        in_specs=[ANY],
        out_specs=ANY,
        scratch_shapes=[pltpu.SemaphoreType.DMA, pltpu.SemaphoreType.DMA],
        compiler_params=pltpu.CompilerParams(collective_id=1, has_side_effects=True),
        name="swap_images",
    )(value)


def backward_kernel(group, reach, foot, live, jac, noise, mine, other, bucket):
    step = pl.program_id(0)

    @pl.when(step == 0)
    def _():
        bucket[...] = jnp.zeros_like(bucket)

    for g in range(group):
        slot = step * group + g
        active = jnp.where(slot < live[0], 1.0, 0.0).astype(jnp.float32)
        scale = noise[pl.ds(slot, 1), :] * active
        weighted = ((mine[g] + other[g]) * scale).astype(jnp.bfloat16)
        for f in range(reach):
            o = foot[slot * reach + f]
            bucket[o] += jnp.dot(weighted, jac[g, f], preferred_element_type=jnp.float32)


def backward(foot, live, jacobian, noise, mine, other, group):
    slots, reach, rows, cells = jacobian.shape
    width = mine.shape[1]
    return pl.pallas_call(
        functools.partial(backward_kernel, group, reach),
        out_shape=jax.ShapeDtypeStruct((REACH, width, cells), jnp.float32),
        grid_spec=pltpu.PrefetchScalarGridSpec(
            num_scalar_prefetch=2,
            grid=(slots // group,),
            in_specs=[
                pl.BlockSpec((group, reach, rows, cells), lambda i, foot, live: (i, 0, 0, 0)),
                pl.BlockSpec((slots, rows), lambda i, foot, live: (0, 0)),
                pl.BlockSpec((group, width, rows), lambda i, foot, live: (i, 0, 0)),
                pl.BlockSpec((group, width, rows), lambda i, foot, live: (i, 0, 0)),
            ],
            out_specs=pl.BlockSpec((REACH, width, cells), lambda i, foot, live: (0, 0, 0)),
        ),
        name="back_project",
    )(foot, live, jacobian, noise, mine, other)


def collect_kernel(bands, split, bucket, probes, field, gram, out_code, out_step, in_code, in_step, half, mine, parts, full, whole,
                   send, recv, gsend, grecv, asend, arecv):
    me, odd, mate, up, down = ring(bands)
    core = lax.axis_index("col")
    partner = {"col": 1 - core}
    peers = [{"tile": lax.rem(me + d, bands)} for d in range(1, bands)]
    greet(peers + [partner])
    straight = {"tile": lax.rem(me + bands - 2 + 4 * odd, bands)}
    turned = {"tile": lax.rem(me + 2 + (bands - 4) * odd, bands)}
    places = [{"tile": mate}, straight, {"tile": mate}, turned]
    hops = [
        (
            remote(out_code.at[i], in_code.at[i], send.at[2 * i], recv.at[2 * i], place),
            remote(out_step.at[i], in_step.at[i], send.at[2 * i + 1], recv.at[2 * i + 1], place),
        )
        for i, place in enumerate(places)
    ]

    def launch(i, term):
        top = jnp.maximum(jnp.max(jnp.abs(term), axis=0, keepdims=True), 1e-30)
        code = jnp.round(term * (LEVELS / top))
        out_code[i] = code.astype(jnp.int32).astype(jnp.int16)
        out_step[i] = jnp.broadcast_to(top * (1.0 / LEVELS), out_step.shape[1:])
        for hop in hops[i]:
            hop.start()

    def arrive(i):
        for hop in hops[i]:
            hop.wait_recv()
        return in_code[i].astype(jnp.int32).astype(jnp.float32) * in_step[i][:1, :]

    launch(0, bucket[1 + 2 * odd])
    launch(1, bucket[4 * odd])
    launch(2, bucket[3 - 2 * odd])
    base = probes[0].astype(jnp.float32).T + bucket[2]
    launch(3, bucket[4 - 4 * odd] + arrive(0))
    base = base + arrive(2)
    base = base + arrive(1)
    field[...] = base + arrive(3)
    for pair in hops:
        for hop in pair:
            hop.wait_send()
    value = field[...]
    local = lax.dot_general(
        value, value, (((1,), (1,)), ((), ())), precision=HIGHEST, preferred_element_type=jnp.float32
    )
    if not split:
        gram[...] = local
        return
    rows = half.shape[1]
    piece = rows // bands
    whole[0] = local[:rows]
    whole[1] = local[rows:]
    hop = remote(whole.at[1 - core], half.at[0], gsend.at[0], grecv.at[0], partner)
    hop.start()
    hop.wait()
    mine[...] = (whole[core] + half[0]).reshape(bands, piece, mine.shape[2])
    hops = []
    for d in range(1, bands):
        target = lax.rem(me + d, bands)
        hops.append(remote(mine.at[target], parts.at[d - 1], gsend.at[d], grecv.at[d], {"tile": target}))
    for hop in hops:
        hop.start()
    total = mine[me]
    for d in range(1, bands):
        hops[d - 1].wait_recv()
        total = total + parts[d - 1]
    for hop in hops:
        hop.wait_send()
    full[me] = total
    hops = []
    for d in range(1, bands):
        target = lax.rem(me + d, bands)
        hops.append(remote(full.at[me], full.at[me], asend.at[d], arecv.at[d], {"tile": target}))
    for hop in hops:
        hop.start()
    for hop in hops:
        hop.wait_recv()
    for hop in hops:
        hop.wait_send()
    hop = remote(full, gram.at[core], asend.at[0], arecv.at[0], partner)
    hop.start()
    gram[core] = full[...]
    hop.wait()


def collect(bucket, probes, bands, split):
    _, width, cells = bucket.shape
    rows = width // 2
    piece = rows // bands if split else 8
    gram_shape = (2, bands, piece, width) if split else (width, width)
    field, gram = pl.pallas_call(
        functools.partial(collect_kernel, bands, split),
        out_shape=(
            jax.ShapeDtypeStruct((width, cells), jnp.float32),
            jax.ShapeDtypeStruct(gram_shape, jnp.float32),
        ),
        in_specs=[VMEM, VMEM],
        out_specs=(VMEM, VMEM),
        scratch_shapes=[
            pltpu.VMEM((4, width, cells), jnp.int16),
            pltpu.VMEM((4, 8, cells), jnp.float32),
            pltpu.VMEM((4, width, cells), jnp.int16),
            pltpu.VMEM((4, 8, cells), jnp.float32),
            pltpu.VMEM((1, rows, width), jnp.float32),
            pltpu.VMEM((bands, piece, width), jnp.float32),
            pltpu.VMEM((bands - 1, piece, width), jnp.float32),
            pltpu.VMEM((bands, piece, width), jnp.float32),
            pltpu.VMEM((2, rows, width), jnp.float32),
            pltpu.SemaphoreType.DMA((8,)),
            pltpu.SemaphoreType.DMA((8,)),
            pltpu.SemaphoreType.DMA((bands,)),
            pltpu.SemaphoreType.DMA((bands,)),
            pltpu.SemaphoreType.DMA((bands,)),
            pltpu.SemaphoreType.DMA((bands,)),
        ],
        compiler_params=pltpu.CompilerParams(collective_id=2, has_side_effects=True),
        name="collect_gram",
    )(bucket, probes)
    return field, gram.reshape(width, width)


def eliminate(pieces):
    size = pieces[0].shape[0]
    lanes = pieces[0].shape[1]
    count = size // 8
    groups = [[piece[8 * g : 8 * g + 8] for piece in pieces] for g in range(count)]
    sub = lax.broadcasted_iota(jnp.int32, (8, lanes), 0)
    for g in range(count):
        panel = groups[g]
        pivots = jnp.ones((8, lanes), jnp.float32)
        for i in range(8):
            j = 8 * g + i
            column = jnp.broadcast_to(panel[0][:, j : j + 1], (8, lanes))
            pivot = jnp.broadcast_to(column[i : i + 1, :], (8, lanes))
            ratio = jnp.where(sub > i, column / pivot, 0.0)
            pivots = jnp.where(sub == i, pivot, pivots)
            panel = [part - ratio * part[i : i + 1, :] for part in panel]
        root = lax.rsqrt(pivots)
        panel = [part * root for part in panel]
        groups[g] = panel
        if g + 1 == count:
            break
        turned = panel[0].T
        for h in range(g + 1, count):
            rest = groups[h]
            for i in range(8):
                lower = jnp.broadcast_to(turned[8 * h : 8 * h + 8, i : i + 1], (8, lanes))
                rest = [r - lower * u[i : i + 1, :] for r, u in zip(rest, panel)]
            groups[h] = rest
    return [
        jnp.concatenate([group[k] for group in groups], axis=0) for k in range(len(pieces))
    ]


def finish_kernel(scale, gram, field, basis, factor, inverse):
    width = gram.shape[0]
    half = width // 2
    row = lax.broadcasted_iota(jnp.int32, (half, half), 0)
    lane = lax.broadcasted_iota(jnp.int32, (half, half), 1)
    unit = jnp.where(row == lane, 1.0, 0.0).astype(jnp.float32)
    keep = lane >= row
    zeros = jnp.zeros((half, half), jnp.float32)
    corner, side, start = eliminate([gram[:half, :half], gram[:half, half:], unit])
    inverse[:half, :half] = start
    inverse[:half, half:] = zeros
    factor[:half, :half] = jnp.where(keep, corner, 0.0) * (1.0 / scale)
    factor[:half, half:] = side * (1.0 / scale)
    across = side.T
    change = jnp.dot(across, side, precision=HIGHEST, preferred_element_type=jnp.float32)
    carry = jnp.dot(across, start, precision=HIGHEST, preferred_element_type=jnp.float32)
    last, below, end = eliminate([gram[half:, half:] - change, -carry, unit])
    inverse[half:, :half] = below
    inverse[half:, half:] = end
    factor[half:, half:] = jnp.where(keep, last, 0.0) * (1.0 / scale)
    factor[half:, :half] = zeros
    solved = jnp.dot(inverse[...], field[...], precision=HIGHEST, preferred_element_type=jnp.float32)
    basis[0] = (solved * scale).T


def finish(gram, field, scale):
    width, cells = field.shape
    return pl.pallas_call(
        functools.partial(finish_kernel, scale),
        out_shape=(
            jax.ShapeDtypeStruct((1, cells, width), jnp.float32),
            jax.ShapeDtypeStruct((width, width), jnp.float32),
        ),
        in_specs=[VMEM, VMEM],
        out_specs=(VMEM, VMEM),
        scratch_shapes=[pltpu.VMEM((width, width), jnp.float32)],
        name="factor_solve",
    )(gram, field)


def on_device(jacobian, footprint, live, noise_weight, probes):
    slots = jacobian.shape[0]
    cells, width = probes.shape[1:]
    bands = lax.axis_size("tile")
    group = math.gcd(slots, 4)
    foot = footprint.reshape(-1)
    split = (width // 2) % (8 * bands) == 0
    window = fetch_window(probes, bands)
    mine = forward(foot, jacobian, window, group)
    other = swap_cores(mine)
    bucket = backward(foot, live, jacobian, noise_weight, mine, other, group)
    field, gram = collect(bucket, probes, bands, split)
    if not split:
        gram = lax.psum(gram, ("tile", "col"))
    scale = math.sqrt(cells * lax.axis_size("col") * bands)
    return finish(gram, field, scale)


def solution(mesh):
    placed = (
        P(("groups", "tile"), None, None, "col"),
        P(("groups", "tile"), None),
        P(("groups", "tile")),
        P(("groups", "tile"), None),
        P(("groups", "tile"), "col", None),
    )
    return jax.shard_map(
        on_device,
        mesh=mesh,
        in_specs=placed,
        out_specs=(P(("groups", "tile"), "col", None), P("groups", None)),
        check_vma=False,
    )
```

```python
import functools
import math

import jax
import jax.numpy as jnp
from jax import lax
from jax.experimental import pallas as pl
from jax.experimental.pallas import tpu as pltpu
from jax.sharding import PartitionSpec as P

MESH = pl.DeviceIdType.MESH
REACH = 5
LEVELS = 32766.0
PARTS = 2
VMEM = pl.BlockSpec(memory_space=pltpu.VMEM)
ANY = pl.BlockSpec(memory_space=pl.ANY)
HIGHEST = lax.Precision.HIGHEST


def remote(src, dst, send, recv, where):
    return pltpu.make_async_remote_copy(
        src_ref=src, dst_ref=dst, send_sem=send, recv_sem=recv,
        device_id=where, device_id_type=MESH,
    )


def greet(devices):
    barrier = pltpu.get_barrier_semaphore()
    for where in devices:
        pl.semaphore_signal(barrier, inc=1, device_id=where, device_id_type=MESH)
    pl.semaphore_wait(barrier, len(devices))


def ring(bands):
    me = lax.axis_index("tile")
    odd = lax.rem(me, 2)
    mate = me + 1 - 2 * odd
    up = lax.rem(me + 2, bands)
    down = lax.rem(me + bands - 2, bands)
    return me, odd, mate, up, down


def images_kernel(bands, group, reach, foot, live, noise, probes, jac, out, held, window, turned,
                  mine, other, load, send, recv, csend, crecv):
    me, odd, mate, up, down = ring(bands)
    partner = {"col": 1 - lax.axis_index("col")}
    slots = jac.shape[0]
    chunks = slots // group
    cells = window.shape[1]
    part = cells // PARTS

    def fetch(c):
        span = pl.ds(c * group, group)
        return pltpu.make_async_copy(jac.at[span], held.at[span], load.at[c])

    def swap(c):
        span = pl.ds(c * group, group)
        return remote(mine.at[span], other.at[span], csend.at[c], crecv.at[c], partner)

    def turn(o):
        turned[o] = window[o].astype(jnp.float32).T.astype(turned.dtype)

    for c in range(chunks):
        fetch(c).start()
    greet([{"tile": mate}, {"tile": up}, {"tile": down}, partner])
    hops = []
    for h in range(PARTS):
        span = pl.ds(h * part, part)
        own = probes.at[0, span]
        hops.append([
            remote(own, window.at[0, span], send.at[h, 0], recv.at[h, 0], {"tile": up}),
            remote(own, window.at[4, span], send.at[h, 1], recv.at[h, 1], {"tile": down}),
            remote(own, window.at[1 + 2 * odd, span], send.at[h, 2], recv.at[h, 2], {"tile": mate}),
            remote(window.at[4 - 4 * odd, span], window.at[3 - 2 * odd, span],
                   send.at[h, 3], recv.at[h, 3], {"tile": mate}),
        ])
    for hop in hops:
        for i in range(3):
            hop[i].start()
    window[2] = probes[0]
    turn(2)
    for h in range(PARTS):
        span = pl.ds(h * part, part)
        remote(probes.at[0, span], window.at[4 - 4 * odd, span], send.at[h, 0],
               recv.at[h, 1 - odd], {"tile": up}).wait_recv()
        hops[h][3].start()
    for h in range(PARTS):
        span = pl.ds(h * part, part)
        hops[h][2].wait_recv()
        remote(probes.at[0, span], window.at[4 * odd, span], send.at[h, 0],
               recv.at[h, odd], {"tile": up}).wait_recv()
    turn(4)
    turn(0)
    for h in range(PARTS):
        hops[h][3].wait_recv()
    turn(1)
    turn(3)

    def step(c, carry):
        fetch(c).wait()
        for g in range(group):
            slot = c * group + g
            total = None
            for f in range(reach):
                o = foot[slot * reach + f]
                term = lax.dot_general(
                    turned[o], held[slot, f], (((1,), (1,)), ((), ())),
                    preferred_element_type=jnp.float32,
                )
                total = term if total is None else total + term
            mine[slot] = total
        swap(c).start()
        return carry

    lax.fori_loop(0, chunks, step, 0)

    def close(c, carry):
        swap(c).wait_recv()
        for g in range(group):
            slot = c * group + g
            active = jnp.where(slot < live[0], 1.0, 0.0).astype(jnp.float32)
            scale = noise[pl.ds(slot, 1), :] * active
            out[slot] = ((mine[slot] + other[slot]) * scale).astype(out.dtype)
        swap(c).wait_send()
        return carry

    lax.fori_loop(0, chunks, close, 0)
    for hop in hops:
        for i in range(4):
            hop[i].wait_send()


def images(foot, live, noise, probes, jacobian, bands, group):
    slots, reach, rows, cells = jacobian.shape
    width = probes.shape[2]
    smem = pl.BlockSpec(memory_space=pltpu.SMEM)
    chunks = slots // group
    return pl.pallas_call(
        functools.partial(images_kernel, bands, group, reach),
        out_shape=jax.ShapeDtypeStruct((slots, width, rows), jnp.bfloat16),
        in_specs=[smem, smem, VMEM, VMEM, ANY],
        out_specs=VMEM,
        scratch_shapes=[
            pltpu.VMEM(jacobian.shape, jacobian.dtype),
            pltpu.VMEM((REACH, cells, width), probes.dtype),
            pltpu.VMEM((REACH, width, cells), probes.dtype),
            pltpu.VMEM((slots, width, rows), jnp.float32),
            pltpu.VMEM((slots, width, rows), jnp.float32),
            pltpu.SemaphoreType.DMA((chunks,)),
            pltpu.SemaphoreType.DMA((PARTS, 4)),
            pltpu.SemaphoreType.DMA((PARTS, 4)),
            pltpu.SemaphoreType.DMA((chunks,)),
            pltpu.SemaphoreType.DMA((chunks,)),
        ],
        compiler_params=pltpu.CompilerParams(
            collective_id=0, has_side_effects=True, vmem_limit_bytes=48 * 1024 * 1024
        ),
        name="weighted_images",
    )(foot, live, noise, probes, jacobian)


def backward_kernel(group, reach, foot, jac, weighted, bucket):
    step = pl.program_id(0)

    @pl.when(step == 0)
    def _():
        bucket[...] = jnp.zeros_like(bucket)

    for g in range(group):
        for f in range(reach):
            o = foot[(step * group + g) * reach + f]
            bucket[o] += jnp.dot(weighted[g], jac[g, f], preferred_element_type=jnp.float32)


def backward(foot, jacobian, weighted, group):
    slots, reach, rows, cells = jacobian.shape
    width = weighted.shape[1]
    return pl.pallas_call(
        functools.partial(backward_kernel, group, reach),
        out_shape=jax.ShapeDtypeStruct((REACH, width, cells), jnp.float32),
        grid_spec=pltpu.PrefetchScalarGridSpec(
            num_scalar_prefetch=1,
            grid=(slots // group,),
            in_specs=[
                pl.BlockSpec((group, reach, rows, cells), lambda i, foot: (i, 0, 0, 0)),
                pl.BlockSpec((group, width, rows), lambda i, foot: (i, 0, 0)),
            ],
            out_specs=pl.BlockSpec((REACH, width, cells), lambda i, foot: (0, 0, 0)),
        ),
        name="back_project",
    )(foot, jacobian, weighted)


def collect_kernel(bands, split, bucket, probes, field, gram, out_code, out_step, in_code, in_step, half, mine, parts, full, whole,
                   send, recv, gsend, grecv, asend, arecv):
    me, odd, mate, up, down = ring(bands)
    core = lax.axis_index("col")
    partner = {"col": 1 - core}
    peers = [{"tile": lax.rem(me + d, bands)} for d in range(1, bands)]
    greet(peers + [partner])
    straight = {"tile": lax.rem(me + bands - 2 + 4 * odd, bands)}
    turned = {"tile": lax.rem(me + 2 + (bands - 4) * odd, bands)}
    places = [{"tile": mate}, straight, {"tile": mate}, turned]
    hops = [
        (
            remote(out_code.at[i], in_code.at[i], send.at[2 * i], recv.at[2 * i], place),
            remote(out_step.at[i], in_step.at[i], send.at[2 * i + 1], recv.at[2 * i + 1], place),
        )
        for i, place in enumerate(places)
    ]

    def launch(i, term):
        top = jnp.maximum(jnp.max(jnp.abs(term), axis=0, keepdims=True), 1e-30)
        code = jnp.round(term * (LEVELS / top))
        out_code[i] = code.astype(jnp.int32).astype(jnp.int16)
        out_step[i] = jnp.broadcast_to(top * (1.0 / LEVELS), out_step.shape[1:])
        for hop in hops[i]:
            hop.start()

    def arrive(i):
        for hop in hops[i]:
            hop.wait_recv()
        return in_code[i].astype(jnp.int32).astype(jnp.float32) * in_step[i][:1, :]

    launch(0, bucket[1 + 2 * odd])
    launch(1, bucket[4 * odd])
    launch(2, bucket[3 - 2 * odd])
    base = probes[0].astype(jnp.float32).T + bucket[2]
    launch(3, bucket[4 - 4 * odd] + arrive(0))
    base = base + arrive(2)
    base = base + arrive(1)
    field[...] = base + arrive(3)
    for pair in hops:
        for hop in pair:
            hop.wait_send()
    value = field[...]
    local = lax.dot_general(
        value, value, (((1,), (1,)), ((), ())), precision=HIGHEST, preferred_element_type=jnp.float32
    )
    if not split:
        gram[...] = local
        return
    rows = half.shape[1]
    piece = rows // bands
    whole[0] = local[:rows]
    whole[1] = local[rows:]
    hop = remote(whole.at[1 - core], half.at[0], gsend.at[0], grecv.at[0], partner)
    hop.start()
    hop.wait()
    mine[...] = (whole[core] + half[0]).reshape(bands, piece, mine.shape[2])
    hops = []
    for d in range(1, bands):
        target = lax.rem(me + d, bands)
        hops.append(remote(mine.at[target], parts.at[d - 1], gsend.at[d], grecv.at[d], {"tile": target}))
    for hop in hops:
        hop.start()
    total = mine[me]
    for d in range(1, bands):
        hops[d - 1].wait_recv()
        total = total + parts[d - 1]
    for hop in hops:
        hop.wait_send()
    full[me] = total
    hops = []
    for d in range(1, bands):
        target = lax.rem(me + d, bands)
        hops.append(remote(full.at[me], full.at[me], asend.at[d], arecv.at[d], {"tile": target}))
    for hop in hops:
        hop.start()
    for hop in hops:
        hop.wait_recv()
    for hop in hops:
        hop.wait_send()
    hop = remote(full, gram.at[core], asend.at[0], arecv.at[0], partner)
    hop.start()
    gram[core] = full[...]
    hop.wait()


def collect(bucket, probes, bands, split):
    _, width, cells = bucket.shape
    rows = width // 2
    piece = rows // bands if split else 8
    gram_shape = (2, bands, piece, width) if split else (width, width)
    field, gram = pl.pallas_call(
        functools.partial(collect_kernel, bands, split),
        out_shape=(
            jax.ShapeDtypeStruct((width, cells), jnp.float32),
            jax.ShapeDtypeStruct(gram_shape, jnp.float32),
        ),
        in_specs=[VMEM, VMEM],
        out_specs=(VMEM, VMEM),
        scratch_shapes=[
            pltpu.VMEM((4, width, cells), jnp.int16),
            pltpu.VMEM((4, 8, cells), jnp.float32),
            pltpu.VMEM((4, width, cells), jnp.int16),
            pltpu.VMEM((4, 8, cells), jnp.float32),
            pltpu.VMEM((1, rows, width), jnp.float32),
            pltpu.VMEM((bands, piece, width), jnp.float32),
            pltpu.VMEM((bands - 1, piece, width), jnp.float32),
            pltpu.VMEM((bands, piece, width), jnp.float32),
            pltpu.VMEM((2, rows, width), jnp.float32),
            pltpu.SemaphoreType.DMA((8,)),
            pltpu.SemaphoreType.DMA((8,)),
            pltpu.SemaphoreType.DMA((bands,)),
            pltpu.SemaphoreType.DMA((bands,)),
            pltpu.SemaphoreType.DMA((bands,)),
            pltpu.SemaphoreType.DMA((bands,)),
        ],
        compiler_params=pltpu.CompilerParams(collective_id=2, has_side_effects=True),
        name="collect_gram",
    )(bucket, probes)
    return field, gram.reshape(width, width)


def eliminate(block):
    size = block.shape[0]
    groups = [block[8 * g : 8 * g + 8] for g in range(size // 8)]
    sub = lax.broadcasted_iota(jnp.int32, (8, 1), 0)
    for g in range(len(groups)):
        panel = groups[g]
        scaled = []
        for i in range(8):
            j = 8 * g + i
            r = lax.rsqrt(panel[i : i + 1, j : j + 1])
            upper = panel[i : i + 1, :] * r
            factor = jnp.where(sub > i, panel[:, j : j + 1] * r, 0.0)
            panel = jnp.where(sub == i, upper, panel - factor * upper)
            scaled.append((j, r, upper))
        groups[g] = panel
        for h in range(g + 1, len(groups)):
            rest = groups[h]
            for j, r, upper in scaled:
                rest = rest - (rest[:, j : j + 1] * r) * upper
            groups[h] = rest
    return jnp.concatenate(groups, axis=0)


def finish_kernel(scale, gram, field, basis, factor, inverse):
    width = gram.shape[0]
    half = width // 2
    row = lax.broadcasted_iota(jnp.int32, (half, half), 0)
    lane = lax.broadcasted_iota(jnp.int32, (half, half), 1)
    unit = jnp.where(row == lane, 1.0, 0.0).astype(jnp.float32)
    keep = lane >= row
    zeros = jnp.zeros((half, half), jnp.float32)
    top = eliminate(jnp.concatenate([gram[:half, :], unit], axis=1))
    side = top[:, half:width]
    inverse[:half, :half] = top[:, width:]
    inverse[:half, half:] = zeros
    factor[:half, :half] = jnp.where(keep, top[:, :half], 0.0) * (1.0 / scale)
    factor[:half, half:] = side * (1.0 / scale)
    change = jnp.dot(side.T, top[:, half:], precision=HIGHEST, preferred_element_type=jnp.float32)
    low = eliminate(
        jnp.concatenate([gram[half:, half:] - change[:, :half], -change[:, half:], unit], axis=1)
    )
    inverse[half:, :] = low[:, half:]
    factor[half:, half:] = jnp.where(keep, low[:, :half], 0.0) * (1.0 / scale)
    factor[half:, :half] = zeros
    solved = jnp.dot(inverse[...], field[...], precision=HIGHEST, preferred_element_type=jnp.float32)
    basis[0] = (solved * scale).T


def finish(gram, field, scale):
    width, cells = field.shape
    return pl.pallas_call(
        functools.partial(finish_kernel, scale),
        out_shape=(
            jax.ShapeDtypeStruct((1, cells, width), jnp.float32),
            jax.ShapeDtypeStruct((width, width), jnp.float32),
        ),
        in_specs=[VMEM, VMEM],
        out_specs=(VMEM, VMEM),
        scratch_shapes=[pltpu.VMEM((width, width), jnp.float32)],
        name="factor_solve",
    )(gram, field)


def on_device(jacobian, footprint, live, noise_weight, probes):
    slots = jacobian.shape[0]
    cells, width = probes.shape[1:]
    bands = lax.axis_size("tile")
    group = math.gcd(slots, 4)
    foot = footprint.reshape(-1)
    split = (width // 2) % (8 * bands) == 0
    weighted = images(foot, live, noise_weight, probes, jacobian, bands, group)
    bucket = backward(foot, jacobian, weighted, group)
    field, gram = collect(bucket, probes, bands, split)
    if not split:
        gram = lax.psum(gram, ("tile", "col"))
    scale = math.sqrt(cells * lax.axis_size("col") * bands)
    return finish(gram, field, scale)


def solution(mesh):
    placed = (
        P(("groups", "tile"), None, None, "col"),
        P(("groups", "tile"), None),
        P(("groups", "tile")),
        P(("groups", "tile"), None),
        P(("groups", "tile"), "col", None),
    )
    return jax.shard_map(
        on_device,
        mesh=mesh,
        in_specs=placed,
        out_specs=(P(("groups", "tile"), "col", None), P("groups", None)),
        check_vma=False,
    )
```

```python
import functools
import math

import jax
import jax.numpy as jnp
from jax import lax
from jax.experimental import pallas as pl
from jax.experimental.pallas import tpu as pltpu
from jax.sharding import PartitionSpec as P

MESH = pl.DeviceIdType.MESH
REACH = 5
LEVELS = 32766.0
PARTS = 2
VMEM = pl.BlockSpec(memory_space=pltpu.VMEM)
ANY = pl.BlockSpec(memory_space=pl.ANY)
HIGHEST = lax.Precision.HIGHEST


def remote(src, dst, send, recv, where):
    return pltpu.make_async_remote_copy(
        src_ref=src, dst_ref=dst, send_sem=send, recv_sem=recv,
        device_id=where, device_id_type=MESH,
    )


def greet(devices):
    barrier = pltpu.get_barrier_semaphore()
    for where in devices:
        pl.semaphore_signal(barrier, inc=1, device_id=where, device_id_type=MESH)
    pl.semaphore_wait(barrier, len(devices))


def ring(bands):
    me = lax.axis_index("tile")
    odd = lax.rem(me, 2)
    mate = me + 1 - 2 * odd
    up = lax.rem(me + 2, bands)
    down = lax.rem(me + bands - 2, bands)
    return me, odd, mate, up, down


def images_kernel(bands, group, reach, foot, live, noise, probes, jac, out, held, window, turned,
                  mine, other, load, send, recv, csend, crecv):
    me, odd, mate, up, down = ring(bands)
    partner = {"col": 1 - lax.axis_index("col")}
    slots = jac.shape[0]
    chunks = slots // group
    cells = window.shape[1]
    part = cells // PARTS

    def fetch(c):
        span = pl.ds(c * group, group)
        return pltpu.make_async_copy(jac.at[span], held.at[span], load.at[c])

    def swap(c):
        span = pl.ds(c * group, group)
        return remote(mine.at[span], other.at[span], csend.at[c], crecv.at[c], partner)

    def turn(o):
        turned[o] = window[o].astype(jnp.float32).T.astype(turned.dtype)

    for c in range(chunks):
        fetch(c).start()
    greet([{"tile": mate}, {"tile": up}, {"tile": down}, partner])
    hops = []
    for h in range(PARTS):
        span = pl.ds(h * part, part)
        own = probes.at[0, span]
        hops.append([
            remote(own, window.at[0, span], send.at[h, 0], recv.at[h, 0], {"tile": up}),
            remote(own, window.at[4, span], send.at[h, 1], recv.at[h, 1], {"tile": down}),
            remote(own, window.at[1 + 2 * odd, span], send.at[h, 2], recv.at[h, 2], {"tile": mate}),
            remote(window.at[4 - 4 * odd, span], window.at[3 - 2 * odd, span],
                   send.at[h, 3], recv.at[h, 3], {"tile": mate}),
        ])
    for hop in hops:
        for i in range(3):
            hop[i].start()
    window[2] = probes[0]
    turn(2)
    for h in range(PARTS):
        span = pl.ds(h * part, part)
        remote(probes.at[0, span], window.at[4 - 4 * odd, span], send.at[h, 0],
               recv.at[h, 1 - odd], {"tile": up}).wait_recv()
        hops[h][3].start()
    for h in range(PARTS):
        span = pl.ds(h * part, part)
        hops[h][2].wait_recv()
        remote(probes.at[0, span], window.at[4 * odd, span], send.at[h, 0],
               recv.at[h, odd], {"tile": up}).wait_recv()
    turn(4)
    turn(0)
    for h in range(PARTS):
        hops[h][3].wait_recv()
    turn(1)
    turn(3)

    def step(c, carry):
        fetch(c).wait()
        for g in range(group):
            slot = c * group + g
            total = None
            for f in range(reach):
                o = foot[slot * reach + f]
                term = lax.dot_general(
                    turned[o], held[slot, f], (((1,), (1,)), ((), ())),
                    preferred_element_type=jnp.float32,
                )
                total = term if total is None else total + term
            mine[slot] = total
        swap(c).start()
        return carry

    lax.fori_loop(0, chunks, step, 0)

    def close(c, carry):
        swap(c).wait_recv()
        for g in range(group):
            slot = c * group + g
            active = jnp.where(slot < live[0], 1.0, 0.0).astype(jnp.float32)
            scale = noise[pl.ds(slot, 1), :] * active
            out[slot] = ((mine[slot] + other[slot]) * scale).astype(out.dtype)
        swap(c).wait_send()
        return carry

    lax.fori_loop(0, chunks, close, 0)
    for hop in hops:
        for i in range(4):
            hop[i].wait_send()


def images(foot, live, noise, probes, jacobian, bands, group):
    slots, reach, rows, cells = jacobian.shape
    width = probes.shape[2]
    smem = pl.BlockSpec(memory_space=pltpu.SMEM)
    chunks = slots // group
    return pl.pallas_call(
        functools.partial(images_kernel, bands, group, reach),
        out_shape=jax.ShapeDtypeStruct((slots, width, rows), jnp.bfloat16),
        in_specs=[smem, smem, VMEM, VMEM, ANY],
        out_specs=VMEM,
        scratch_shapes=[
            pltpu.VMEM(jacobian.shape, jacobian.dtype),
            pltpu.VMEM((REACH, cells, width), probes.dtype),
            pltpu.VMEM((REACH, width, cells), probes.dtype),
            pltpu.VMEM((slots, width, rows), jnp.float32),
            pltpu.VMEM((slots, width, rows), jnp.float32),
            pltpu.SemaphoreType.DMA((chunks,)),
            pltpu.SemaphoreType.DMA((PARTS, 4)),
            pltpu.SemaphoreType.DMA((PARTS, 4)),
            pltpu.SemaphoreType.DMA((chunks,)),
            pltpu.SemaphoreType.DMA((chunks,)),
        ],
        compiler_params=pltpu.CompilerParams(
            collective_id=0, has_side_effects=True, vmem_limit_bytes=48 * 1024 * 1024
        ),
        name="weighted_images",
    )(foot, live, noise, probes, jacobian)


def backward_kernel(group, reach, foot, jac, weighted, bucket):
    step = pl.program_id(0)

    @pl.when(step == 0)
    def _():
        bucket[...] = jnp.zeros_like(bucket)

    for g in range(group):
        for f in range(reach):
            o = foot[(step * group + g) * reach + f]
            bucket[o] += jnp.dot(weighted[g], jac[g, f], preferred_element_type=jnp.float32)


def backward(foot, jacobian, weighted, group):
    slots, reach, rows, cells = jacobian.shape
    width = weighted.shape[1]
    return pl.pallas_call(
        functools.partial(backward_kernel, group, reach),
        out_shape=jax.ShapeDtypeStruct((REACH, width, cells), jnp.float32),
        grid_spec=pltpu.PrefetchScalarGridSpec(
            num_scalar_prefetch=1,
            grid=(slots // group,),
            in_specs=[
                pl.BlockSpec((group, reach, rows, cells), lambda i, foot: (i, 0, 0, 0)),
                pl.BlockSpec((group, width, rows), lambda i, foot: (i, 0, 0)),
            ],
            out_specs=pl.BlockSpec((REACH, width, cells), lambda i, foot: (0, 0, 0)),
        ),
        name="back_project",
    )(foot, jacobian, weighted)


def collect_kernel(bands, split, bucket, probes, field, gram, out_code, out_step, in_code, in_step, half, mine, parts, full, whole,
                   send, recv, gsend, grecv, asend, arecv, fsend, frecv):
    me, odd, mate, up, down = ring(bands)
    core = lax.axis_index("col")
    partner = {"col": 1 - core}
    peers = [{"tile": lax.rem(me + d, bands)} for d in range(1, bands)]
    greet(peers + [partner])
    straight = {"tile": lax.rem(me + bands - 2 + 4 * odd, bands)}
    turned = {"tile": lax.rem(me + 2 + (bands - 4) * odd, bands)}
    places = [{"tile": mate}, straight, {"tile": mate}, turned]
    hops = [
        (
            remote(out_code.at[i], in_code.at[i], send.at[2 * i], recv.at[2 * i], place),
            remote(out_step.at[i], in_step.at[i], send.at[2 * i + 1], recv.at[2 * i + 1], place),
        )
        for i, place in enumerate(places)
    ]

    def launch(i, term):
        top = jnp.maximum(jnp.max(jnp.abs(term), axis=0, keepdims=True), 1e-30)
        code = jnp.round(term * (LEVELS / top))
        out_code[i] = code.astype(jnp.int32).astype(jnp.int16)
        out_step[i] = jnp.broadcast_to(top * (1.0 / LEVELS), out_step.shape[1:])
        for hop in hops[i]:
            hop.start()

    def arrive(i):
        for hop in hops[i]:
            hop.wait_recv()
        return in_code[i].astype(jnp.int32).astype(jnp.float32) * in_step[i][:1, :]

    launch(0, bucket[1 + 2 * odd])
    launch(1, bucket[4 * odd])
    launch(2, bucket[3 - 2 * odd])
    base = probes[0].astype(jnp.float32).T + bucket[2]
    launch(3, bucket[4 - 4 * odd] + arrive(0))
    base = base + arrive(2)
    base = base + arrive(1)
    field[...] = base + arrive(3)
    for pair in hops:
        for hop in pair:
            hop.wait_send()
    value = field[...]
    local = lax.dot_general(
        value, value, (((1,), (1,)), ((), ())), precision=HIGHEST, preferred_element_type=jnp.float32
    )
    if not split:
        gram[...] = local
        return
    rows = half.shape[1]
    piece = rows // bands
    whole[0] = local[:rows]
    whole[1] = local[rows:]
    hop = remote(whole.at[1 - core], half.at[0], gsend.at[0], grecv.at[0], partner)
    hop.start()
    hop.wait()
    mine[...] = (whole[core] + half[0]).reshape(bands, piece, mine.shape[2])
    hops = []
    for d in range(1, bands):
        target = lax.rem(me + d, bands)
        hops.append(remote(mine.at[target], parts.at[d - 1], gsend.at[d], grecv.at[d], {"tile": target}))
    for hop in hops:
        hop.start()
    total = mine[me]
    for d in range(1, bands):
        hops[d - 1].wait_recv()
        total = total + parts[d - 1]
    for hop in hops:
        hop.wait_send()
    full[me] = total
    hops = []
    for d in range(1, bands):
        target = lax.rem(me + d, bands)
        hops.append(remote(full.at[me], full.at[me], asend.at[d], arecv.at[d], {"tile": target}))
    for hop in hops:
        hop.start()
    shares = [remote(full.at[me], gram.at[core, me], fsend.at[0], frecv.at[0], partner)]
    shares[0].start()
    for d in range(1, bands):
        source = lax.rem(me + bands - d, bands)
        hops[d - 1].wait_recv()
        shares.append(
            remote(full.at[source], gram.at[core, source], fsend.at[d], frecv.at[d], partner)
        )
        shares[d].start()
    gram[core] = full[...]
    for hop in hops:
        hop.wait_send()
    for share in shares:
        share.wait()


def collect(bucket, probes, bands, split):
    _, width, cells = bucket.shape
    rows = width // 2
    piece = rows // bands if split else 8
    gram_shape = (2, bands, piece, width) if split else (width, width)
    field, gram = pl.pallas_call(
        functools.partial(collect_kernel, bands, split),
        out_shape=(
            jax.ShapeDtypeStruct((width, cells), jnp.float32),
            jax.ShapeDtypeStruct(gram_shape, jnp.float32),
        ),
        in_specs=[VMEM, VMEM],
        out_specs=(VMEM, VMEM),
        scratch_shapes=[
            pltpu.VMEM((4, width, cells), jnp.int16),
            pltpu.VMEM((4, 8, cells), jnp.float32),
            pltpu.VMEM((4, width, cells), jnp.int16),
            pltpu.VMEM((4, 8, cells), jnp.float32),
            pltpu.VMEM((1, rows, width), jnp.float32),
            pltpu.VMEM((bands, piece, width), jnp.float32),
            pltpu.VMEM((bands - 1, piece, width), jnp.float32),
            pltpu.VMEM((bands, piece, width), jnp.float32),
            pltpu.VMEM((2, rows, width), jnp.float32),
            pltpu.SemaphoreType.DMA((8,)),
            pltpu.SemaphoreType.DMA((8,)),
            pltpu.SemaphoreType.DMA((bands,)),
            pltpu.SemaphoreType.DMA((bands,)),
            pltpu.SemaphoreType.DMA((bands,)),
            pltpu.SemaphoreType.DMA((bands,)),
            pltpu.SemaphoreType.DMA((bands,)),
            pltpu.SemaphoreType.DMA((bands,)),
        ],
        compiler_params=pltpu.CompilerParams(collective_id=2, has_side_effects=True),
        name="collect_gram",
    )(bucket, probes)
    return field, gram.reshape(width, width)


def eliminate(block):
    size = block.shape[0]
    groups = [block[8 * g : 8 * g + 8] for g in range(size // 8)]
    sub = lax.broadcasted_iota(jnp.int32, (8, 1), 0)
    for g in range(len(groups)):
        panel = groups[g]
        scaled = []
        for i in range(8):
            j = 8 * g + i
            r = lax.rsqrt(panel[i : i + 1, j : j + 1])
            upper = panel[i : i + 1, :] * r
            factor = jnp.where(sub > i, panel[:, j : j + 1] * r, 0.0)
            panel = jnp.where(sub == i, upper, panel - factor * upper)
            scaled.append((j, r, upper))
        groups[g] = panel
        for h in range(g + 1, len(groups)):
            rest = groups[h]
            for j, r, upper in scaled:
                rest = rest - (rest[:, j : j + 1] * r) * upper
            groups[h] = rest
    return jnp.concatenate(groups, axis=0)


def finish_kernel(scale, gram, field, basis, factor, inverse):
    width = gram.shape[0]
    half = width // 2
    row = lax.broadcasted_iota(jnp.int32, (half, half), 0)
    lane = lax.broadcasted_iota(jnp.int32, (half, half), 1)
    unit = jnp.where(row == lane, 1.0, 0.0).astype(jnp.float32)
    keep = lane >= row
    zeros = jnp.zeros((half, half), jnp.float32)
    top = eliminate(jnp.concatenate([gram[:half, :], unit], axis=1))
    side = top[:, half:width]
    inverse[:half, :half] = top[:, width:]
    inverse[:half, half:] = zeros
    factor[:half, :half] = jnp.where(keep, top[:, :half], 0.0) * (1.0 / scale)
    factor[:half, half:] = side * (1.0 / scale)
    change = jnp.dot(side.T, top[:, half:], precision=HIGHEST, preferred_element_type=jnp.float32)
    low = eliminate(
        jnp.concatenate([gram[half:, half:] - change[:, :half], -change[:, half:], unit], axis=1)
    )
    inverse[half:, :] = low[:, half:]
    factor[half:, half:] = jnp.where(keep, low[:, :half], 0.0) * (1.0 / scale)
    factor[half:, :half] = zeros
    solved = jnp.dot(inverse[...], field[...], precision=HIGHEST, preferred_element_type=jnp.float32)
    basis[0] = (solved * scale).T


def finish(gram, field, scale):
    width, cells = field.shape
    return pl.pallas_call(
        functools.partial(finish_kernel, scale),
        out_shape=(
            jax.ShapeDtypeStruct((1, cells, width), jnp.float32),
            jax.ShapeDtypeStruct((width, width), jnp.float32),
        ),
        in_specs=[VMEM, VMEM],
        out_specs=(VMEM, VMEM),
        scratch_shapes=[pltpu.VMEM((width, width), jnp.float32)],
        name="factor_solve",
    )(gram, field)


def on_device(jacobian, footprint, live, noise_weight, probes):
    slots = jacobian.shape[0]
    cells, width = probes.shape[1:]
    bands = lax.axis_size("tile")
    group = math.gcd(slots, 4)
    foot = footprint.reshape(-1)
    split = (width // 2) % (8 * bands) == 0
    weighted = images(foot, live, noise_weight, probes, jacobian, bands, group)
    bucket = backward(foot, jacobian, weighted, group)
    field, gram = collect(bucket, probes, bands, split)
    if not split:
        gram = lax.psum(gram, ("tile", "col"))
    scale = math.sqrt(cells * lax.axis_size("col") * bands)
    return finish(gram, field, scale)


def solution(mesh):
    placed = (
        P(("groups", "tile"), None, None, "col"),
        P(("groups", "tile"), None),
        P(("groups", "tile")),
        P(("groups", "tile"), None),
        P(("groups", "tile"), "col", None),
    )
    return jax.shard_map(
        on_device,
        mesh=mesh,
        in_specs=placed,
        out_specs=(P(("groups", "tile"), "col", None), P("groups", None)),
        check_vma=False,
    )
```
